128 devices in a mesh: row: 16 (over y, z_hi, core), col: 8 (over z_lo, x).
Axes of the slice: x: 4, y: 4, z: 4 (z_hi: 2, z_lo: 2; z = z_hi * 2 + z_lo), core: 2. Of those that a mesh axis runs over, the one named last changes fastest.
Arguments:
- tokens: bfloat16 [16384, 5120], P('row'), may hold values from -6 to 6
- cotangent: bfloat16 [16384, 4096], P('row', 'col'), may hold values from -0.099609375 to 0.099609375
- small_weight: bfloat16 [2560, 4096], P(None, 'col'), may hold values from -0.125 to 0.125
- expand_in: bfloat16 [5120, 2560], P('row'), may hold values from -0.125 to 0.125
- expand_out: bfloat16 [4096, 4096], P('row', 'col'), may hold values from -0.09375 to 0.09375
Outputs:
- projected: bfloat16 [16384, 4096], P('row', 'col')
- grad_grown: float32 [5120, 4096], P('row', 'col')
- grad_in: float32 [5120, 2560], P('row', 'col')
- grad_out: float32 [4096, 4096], P('row', 'col')
The draws below stay inside these ranges and needn't reach their ends.
All inputs are finite; a program needn't handle non-finite values.
Results may differ from the reference program's by a relative error of at most 0.014.
Values may be sent and summed in bfloat16 or wider, within the bound.
No kernel may reach another device: no remote copies, remote signals or barrier semaphores. Data moves between devices by JAX's collectives and lax.ppermute only.
A program may use at most 128 MiB of HBM per device.

```python
import jax
import jax.numpy as jnp
from jax import lax

DM = 5120
DS = 2560
QS = 4096
QL = 4096
TOKENS = 16384


def levels(key, extent, cuts, least, largest):
    def one(position, parts):
        heights = jax.random.uniform(jax.random.fold_in(jax.random.fold_in(key, 6), position), (parts,), jnp.float32, least / len(cuts), largest / len(cuts))
        return jnp.repeat(jnp.exp(heights), extent[position] // parts).reshape((-1,) + (1,) * (len(extent) - position - 1))

    level = one(*cuts[0])
    for cut in cuts[1:]:
        level = level * one(*cut)
    return level


def centred(stream_key, shape, deviation, most, pieces=(), held_as=jnp.bfloat16):
    factor_of = levels(stream_key, shape, pieces, -0.22, 0.18) if pieces else 1.0
    entries = jax.random.normal(stream_key, shape, jnp.float32) * deviation * factor_of
    return jnp.minimum(jnp.maximum(entries, -most), most).astype(held_as)


def setup_inputs(seed: int = 0) -> dict:
    splits = jax.random.split(jax.random.key(seed), 6)
    return {
        "tokens": centred(splits[0], (TOKENS, DM), 1.0, 6.0, ((0, 16),)),
        "cotangent": centred(splits[1], (TOKENS, QL), 0.015625, 0.099609375, ((0, 16), (1, 8))),
        "small_weight": centred(splits[2], (DS, QS), DS ** -0.5, 0.125, ((1, 8),)),
        "expand_in": centred(splits[3], (DM, DS), DS ** -0.5, 0.125, ((0, 16),)),
        "expand_out": centred(splits[4], (QS, QL), QS ** -0.5, 0.09375, ((0, 16), (1, 8))),
    }


def reference(tokens, cotangent, small_weight, expand_in, expand_out):
    mixed = jnp.dot(expand_in, small_weight, preferred_element_type=jnp.float32).astype(jnp.bfloat16)
    grown = jnp.dot(mixed, expand_out, preferred_element_type=jnp.float32).astype(jnp.bfloat16)
    projected = jnp.dot(tokens, grown, preferred_element_type=jnp.float32).astype(jnp.bfloat16)
    grad_grown = lax.dot_general(tokens, cotangent, (((0,), (0,)), ((), ())), preferred_element_type=jnp.float32)
    grad_low = grad_grown.astype(jnp.bfloat16)
    back = lax.dot_general(grad_low, expand_out, (((1,), (1,)), ((), ())), preferred_element_type=jnp.float32).astype(jnp.bfloat16)
    grad_in = lax.dot_general(back, small_weight, (((1,), (1,)), ((), ())), preferred_element_type=jnp.float32)
    grad_out = lax.dot_general(mixed, grad_low, (((0,), (0,)), ((), ())), preferred_element_type=jnp.float32)
    return projected, grad_grown, grad_in, grad_out
```

```python
import jax
import jax.numpy as jnp
from jax import lax
from jax.sharding import Mesh
from jax.sharding import PartitionSpec as P

ROW = ("y", "zh", "core")
COL = ("zl", "x")
SIZES = {"y": 4, "zh": 2, "core": 2, "zl": 2, "x": 4}
BF16 = jnp.bfloat16
F32 = jnp.float32


def shift(array, axis, by):
    size = SIZES[axis]
    return lax.ppermute(array, axis, [(i, (i + by) % size) for i in range(size)])


def dot(a, b, dims, to=BF16):
    return lax.dot_general(a, b, (dims, ((), ())), preferred_element_type=F32).astype(to)


def gathered(own, pair, ring):
    other = shift(own, pair, 1)
    here = jnp.stack([own, other])
    below = shift(here, ring, 1)
    above = shift(here, ring, -1)
    far = jnp.stack([shift(below[0], ring, 1), shift(above[1], ring, -1)])
    return here, above, far, below


def reduced(part, pair, ring):
    a = shift(part(2, 0), ring, 1)
    b = shift(part(2, 1), ring, -1)
    up = shift(jnp.stack([part(1, 0) + a, part(1, 1)]), ring, 1)
    down = shift(jnp.stack([part(3, 0), part(3, 1) + b]), ring, -1)
    sums = [
        part(0, i).astype(F32) + up[i].astype(F32) + down[i].astype(F32) for i in range(2)
    ]
    return sums[0] + shift(sums[1].astype(BF16), pair, 1).astype(F32)


def both_cores(mine, core):
    theirs = shift(mine, "core", 1)
    first = core == 0
    return jnp.concatenate([jnp.where(first, mine, theirs), jnp.where(first, theirs, mine)], 1)


def body(tokens, cotangent, small_weight, expand_in, expand_out):
    y, zh, core, zl, x = (lax.axis_index(a) for a in ("y", "zh", "core", "zl", "x"))
    row = (y * 2 + zh) * 2 + core

    def row_chip(dy, dz):
        return lax.rem(y + dy, 4) * 2 + lax.rem(zh + dz, 2)

    def col_chip(dx, dz):
        return lax.rem(zl + dz, 2) * 4 + lax.rem(x + dx, 4)

    def row_place(chip):
        return lax.rem(chip // 2 - y + 4, 4) * 2 + lax.rem(chip + zh, 2)

    def col_place(chip):
        return lax.rem(chip - x + 4, 4) * 2 + lax.rem(chip // 4 + zl, 2)

    def at(array, index):
        return lax.dynamic_index_in_dim(array, index, 0, keepdims=False)

    out_blocks = gathered(expand_out, "zh", "y")
    rows = small_weight.shape[0] // 16
    slice_blocks = gathered(lax.dynamic_slice_in_dim(small_weight, row * rows, rows, 0), "zl", "x")
    mixed_part = dot(expand_in, small_weight, ((1,), (0,)))
    mixed_blocks = gathered(mixed_part, "zl", "x")

    partial = dot(tokens, cotangent, ((0,), (0,)))
    partial = partial.reshape(8, 2, 320, 512)
    sent = lax.dynamic_index_in_dim(partial, 1 - core, 1, keepdims=False)
    kept = lax.dynamic_index_in_dim(partial, core, 1, keepdims=False)
    kept = kept + shift(sent, "core", 1)
    grad_grown = reduced(lambda dy, dz: at(kept, row_chip(dy, dz)), "zh", "y")
    grad_low = grad_grown.astype(BF16)

    out_panel = jnp.concatenate([both_cores(pair, core) for pair in out_blocks])
    out_panel = jnp.concatenate(
        [at(out_panel, row_place(col_chip(dx, dz))) for dx in range(4) for dz in range(2)]
    )
    slice_panel = jnp.concatenate([b for pair in slice_blocks for b in pair], 1)
    mixed_panel = jnp.concatenate(mixed_blocks)
    flat_mixed = jnp.concatenate([b for pair in mixed_blocks for b in pair], 1)

    through_slice = dot(slice_panel, out_panel, ((1,), (0,)))
    grown = dot(flat_mixed, out_panel, ((1,), (0,)))
    through = jnp.concatenate(
        [both_cores(pair, core) for pair in gathered(through_slice, "zh", "y")]
    )

    in_part = dot(through, grad_low, ((2,), (1,)))
    grad_in = reduced(lambda dx, dz: at(in_part, row_place(col_chip(dx, dz))), "zl", "x").T

    out_part = dot(mixed_panel, grad_low, ((1,), (0,))).reshape(8, 2, 256, 512)
    sent = lax.dynamic_index_in_dim(out_part, 1 - core, 1, keepdims=False)
    kept_out = lax.dynamic_index_in_dim(out_part, core, 1, keepdims=False)
    kept_out = kept_out + shift(sent, "core", 1)
    grad_out = reduced(lambda dy, dz: at(kept_out, col_place(row_chip(dy, dz))), "zh", "y")

    total = None
    for dy, pair in enumerate(gathered(grown, "zh", "y")):
        same, other = both_cores(pair, core)
        first = zh == 0
        group = jnp.concatenate([jnp.where(first, same, other), jnp.where(first, other, same)])
        features = lax.dynamic_slice_in_dim(tokens, lax.rem(y + dy, 4) * 1280, 1280, 1)
        term = dot(features, group, ((1,), (0,)), F32)
        total = term if total is None else total + term
    return total.astype(BF16), grad_grown, grad_in, grad_out


def solution(mesh):
    split = Mesh(mesh.devices.reshape(4, 2, 2, 2, 4), ("y", "zh", "core", "zl", "x"))
    in_specs = (P(ROW, None), P(ROW, COL), P(None, COL), P(ROW, None), P(ROW, COL))
    out_specs = (P(ROW, COL), P(ROW, COL), P(ROW, COL), P(ROW, COL))
    return jax.shard_map(body, mesh=split, in_specs=in_specs, out_specs=out_specs, check_vma=False)
```
